256 devices in a mesh: level: 4 (over z_lo, core), tile: 64 (over x, z_hi, y).
Axes of the slice: x: 4, y: 4, z: 8 (z_hi: 4, z_lo: 2; z = z_hi * 2 + z_lo), core: 2. Of those that a mesh axis runs over, the one named last changes fastest.
Arguments:
- queue_init: bfloat16 [4, 4, 4, 256, 128], P('level', None, None, 'tile'), may hold values from -6 to 6
- noise_frames: bfloat16 [2, 4, 4, 256, 128], P(None, None, None, 'tile'), may hold values from -6 to 6
- conv_first: bfloat16 [3, 3, 320, 4], replicated, may hold values from -1 to 1
- conv_second: bfloat16 [3, 3, 320, 320], replicated, may hold values from -0.109375 to 0.109375
- time_weight: bfloat16 [3, 320, 320], replicated, may hold values from -0.1875 to 0.1875
- out_proj: bfloat16 [4, 320], replicated, may hold values from -0.3125 to 0.3125
- keep_coef: float32 [2, 4, 4], replicated, may hold values from 0.6 to 1
- noise_coef: float32 [2, 4, 4], replicated, may hold values from 0.1 to 0.5
Outputs:
- queue_final: bfloat16 [4, 4, 4, 256, 128], P('level', None, None, 'tile')
The draws below stay inside these ranges and needn't reach their ends.
All inputs are finite; a program needn't handle non-finite values.
Results may differ from the reference program's by a relative error of at most 0.0048.
Values may be sent and summed in bfloat16 or wider, within the bound.
A program may use at most 64 MiB of HBM per device.

```python
import math
import jax
import jax.numpy as jnp
from jax import lax

CHANNELS = 320
LATENT = 4
FRAMES = 4
WIDTH = 128
STEPS = 2
GROUPS = 4
HEIGHT = 256


def block_levels(own_key, extent, pieces, low, largest):
    def one(position, shards_of):
        heights = jax.random.uniform(jax.random.fold_in(jax.random.fold_in(own_key, 6), position), (shards_of,), jnp.float32, low / len(pieces), largest / len(pieces))
        return jnp.repeat(jnp.exp(heights), extent[position] // shards_of).reshape((-1,) + (1,) * (len(extent) - position - 1))

    loudness = one(*pieces[0])
    for cut in pieces[1:]:
        loudness = loudness * one(*cut)
    return loudness


def centred(own_key, dims, scale, limit, pieces=(), held_as=jnp.bfloat16):
    gain = block_levels(own_key, dims, pieces, -0.22, 0.18) if pieces else 1.0
    array = jax.random.normal(own_key, dims, jnp.float32) * scale * gain
    return jnp.minimum(jnp.maximum(array, -limit), limit).astype(held_as)


def setup_inputs(seed: int = 0) -> dict:
    key_of = jax.random.split(jax.random.key(seed), 9)
    queue_init = centred(key_of[0], (GROUPS, FRAMES, LATENT, HEIGHT, WIDTH), 1.0, 6.0, ((0, 4), (3, 64)))
    noise_frames = centred(key_of[1], (STEPS, FRAMES, LATENT, HEIGHT, WIDTH), 1.0, 6.0, ((3, 64),))
    conv_first = centred(key_of[2], (3, 3, CHANNELS, LATENT), (9 * LATENT) ** -0.5, 1.0)
    conv_second = centred(key_of[3], (3, 3, CHANNELS, CHANNELS), (9 * CHANNELS) ** -0.5, 0.109375)
    time_weight = centred(key_of[4], (3, CHANNELS, CHANNELS), (3 * CHANNELS) ** -0.5, 0.1875)
    out_proj = centred(key_of[5], (LATENT, CHANNELS), CHANNELS ** -0.5, 0.3125)
    keep_coef = jnp.clip(jnp.exp(jax.random.uniform(key_of[6], (STEPS, GROUPS, FRAMES), jnp.float32, math.log(0.6), math.log(1.0))), 0.6, 1.0)
    noise_coef = jnp.clip(jnp.exp(jax.random.uniform(key_of[7], (STEPS, GROUPS, FRAMES), jnp.float32, math.log(0.1), math.log(0.5))), 0.1, 0.5)
    return dict(queue_init=queue_init, noise_frames=noise_frames, conv_first=conv_first, conv_second=conv_second, time_weight=time_weight, out_proj=out_proj, keep_coef=keep_coef, noise_coef=noise_coef)


def conv_frames(frames, weight):
    padded = jnp.pad(frames.astype(jnp.float32), ((0, 0), (0, 0), (1, 1), (1, 1)))
    weight_full = weight.astype(jnp.float32)
    height_now = frames.shape[2]
    width_now = frames.shape[3]
    running = jnp.zeros((frames.shape[0], weight.shape[2], height_now, width_now), jnp.float32)
    for row_tap in range(3):
        for col_tap in range(3):
            window = padded[:, :, row_tap:row_tap + height_now, col_tap:col_tap + width_now]
            running = running + jnp.einsum('oc,fchw->fohw', weight_full[row_tap, col_tap], window)
    return running


def reference(queue_init, noise_frames, conv_first, conv_second, time_weight, out_proj, keep_coef, noise_coef):
    queued = queue_init
    time_full = time_weight.astype(jnp.float32)
    proj_full = out_proj.astype(jnp.float32)
    for step_index in range(STEPS):
        queued = jnp.concatenate([noise_frames[step_index][None], queued[:-1]], axis=0)
        first_act = lax.map(lambda group: jax.nn.silu(conv_frames(group, conv_first)).astype(jnp.bfloat16), queued)
        second = lax.map(lambda group: conv_frames(group, conv_second), first_act)
        active = jax.nn.silu(second).astype(jnp.bfloat16)
        flat = active.reshape((GROUPS * FRAMES,) + active.shape[2:])
        padded = jnp.pad(flat, ((1, 1), (0, 0), (0, 0), (0, 0)))

        def temporal_group(group_index):
            window = lax.dynamic_slice_in_dim(padded, group_index * FRAMES, FRAMES + 2, 0).astype(jnp.float32)
            running = jnp.einsum('oc,fchw->fohw', time_full[0], window[0:FRAMES])
            running = running + jnp.einsum('oc,fchw->fohw', time_full[1], window[1:FRAMES + 1])
            running = running + jnp.einsum('oc,fchw->fohw', time_full[2], window[2:FRAMES + 2])
            return running

        temporal = lax.map(temporal_group, jnp.arange(GROUPS, dtype=jnp.int32))
        predicted = (second + temporal).astype(jnp.bfloat16)
        projected = lax.map(lambda group: jnp.einsum('oc,fchw->fohw', proj_full, group.astype(jnp.float32)), predicted)
        keep_rate = keep_coef[step_index][:, :, None, None, None]
        noise_rate = noise_coef[step_index][:, :, None, None, None]
        queued = (keep_rate * queued.astype(jnp.float32) - noise_rate * projected).astype(jnp.bfloat16)
    return queued
```

```python
import functools

import jax
import jax.numpy as jnp
from jax import lax
from jax.experimental import pallas as pl
from jax.experimental.pallas import tpu as pltpu
from jax.sharding import PartitionSpec as P

STEPS = 2
CH = 320
COLS = 128
ORDER = (0, 3, 1, 2)
F32 = jnp.float32
BF16 = jnp.bfloat16
MESH = pl.DeviceIdType.MESH


def block_of(frame):
    return ORDER.index(frame)


def shifted_cols(value, amount):
    lane = lax.broadcasted_iota(jnp.int32, value.shape, 1)
    rolled = pltpu.roll(value, amount % COLS, 1)
    edge = 0 if amount == 1 else COLS - 1
    return jnp.where(lane == edge, jnp.zeros_like(rolled), rolled)


def spread(source, index, target, base):
    for frame in range(4):
        for channel in range(4):
            piece = source[index + (frame, channel)].astype(F32)
            target[block_of(frame), pl.ds(base + channel, 4, stride=4), :] = piece


def prepare_first(cf, w1t, w1, top_mask, bottom_mask):
    w1t[...] = jnp.zeros_like(w1t)
    for row_tap in range(3):
        for col_tap in range(3):
            place = col_tap * 32 + row_tap * 4
            w1t[place : place + 4, 0:CH] = cf[row_tap * 3 + col_tap].astype(F32) * 0.5
    base = jnp.transpose(w1t[...])[0:CH]
    for row in range(6):
        value = pltpu.roll(base, 4 * row, 1) if row else base
        if row == 0:
            value = value * top_mask
        if row == 5:
            value = value * bottom_mask
        w1[row * CH : (row + 1) * CH, :] = value.astype(BF16)


def prepare_second(cs, wcat):
    for tap in range(9):
        wcat[:, tap * CH : (tap + 1) * CH] = cs[tap] * jnp.asarray(0.5, BF16)


def prepare_projection(op, tw, p16, pst):
    p16[...] = jnp.zeros_like(p16)
    p16[0:4, :] = op[...].astype(F32)
    p16[12:16, :] = op[...].astype(F32)
    both = p16[...].astype(BF16)
    pst[...] = jnp.zeros_like(pst)
    through = [jnp.dot(both, tw[k], preferred_element_type=F32) for k in range(3)]
    for odd in range(2):
        rows = slice(odd * 8, odd * 8 + 8)
        pst[odd, 0:8, 0:CH] = p16[rows, :] * 2.0
        for place, k in enumerate((1, 0, 2)):
            pst[odd, place * 8 : place * 8 + 8, 384 : 384 + CH] = through[k][rows]


def window_columns(q, x1):
    for block in range(4):
        lanes = slice(block * COLS, (block + 1) * COLS)
        value = q[block]
        x1[0:32, lanes] = shifted_cols(value, 1).astype(BF16)
        x1[32:64, lanes] = value.astype(BF16)
        x1[64:96, lanes] = shifted_cols(value, -1).astype(BF16)


def first_row(row, pair, x1, w1, stack):
    half = jnp.dot(
        w1[row * CH : (row + 1) * CH, 0:96], x1[:, pair * 256 : pair * 256 + 256], preferred_element_type=F32
    )
    act = half + half * jnp.tanh(half)
    for block in range(2):
        lanes = slice(block * COLS, (block + 1) * COLS)
        piece = act[:, lanes]
        base = row * 3 * CH
        stack[pair, base : base + CH, lanes] = shifted_cols(piece, 1).astype(BF16)
        stack[pair, base + CH : base + 2 * CH, lanes] = piece.astype(BF16)
        stack[pair, base + 2 * CH : base + 3 * CH, lanes] = shifted_cols(piece, -1).astype(BF16)


def second_row(row, pair, wcat, stack, pst, held, sums):
    half = jnp.dot(
        wcat[...], stack[pair, row * 3 * CH : (row + 3) * 3 * CH, :], preferred_element_type=F32
    )
    slot = pair * 4 + row
    held[slot, 0:CH, :] = half.astype(BF16)
    held[slot, 384 : 384 + CH, :] = (half + half * jnp.tanh(half)).astype(BF16)
    terms = jnp.dot(pst[row % 2].astype(BF16), held[slot], preferred_element_type=F32)
    rows = slice(8 * (row // 2), 8 * (row // 2) + 8)
    for place in range(3):
        term = terms[place * 8 : place * 8 + 8]
        if row % 2:
            sums[pair, place, rows, :] += term
        else:
            sums[pair, place, rows, :] = term


def part(sums, place, frame):
    block = block_of(frame)
    return sums[block // 2, place, :, (block % 2) * COLS : (block % 2 + 1) * COLS]


def kernel(levels, tiles, comm, queue_hbm, noise_hbm, cf_hbm, cs_hbm, tw_hbm, op_hbm, keep, rate, out,
           qin, nin, cf, cs, tw, op, wcat, w1t, w1, p16, pst, q, stage, x1, stack, held, sums,
           lo_send, hi_send, lo_recv, hi_recv, load_sem, send_sem, recv_sem):
    if comm:
        g, t = lax.axis_index("level"), lax.axis_index("tile")
    else:
        g, t = jnp.int32(0), jnp.int32(1)

    loads = [
        pltpu.make_async_copy(source, target, load_sem.at[i])
        for i, (source, target) in enumerate(
            [(queue_hbm, qin), (noise_hbm, nin), (cf_hbm, cf), (op_hbm, op), (tw_hbm, tw), (cs_hbm, cs)]
        )
    ]
    for load in loads:
        load.start()

    has_up, has_down = t > 0, t < tiles - 1
    not_last = g < levels - 1

    if comm:
        barrier = pltpu.get_barrier_semaphore()
        count = jnp.int32(0)
        for dg in (-1, 0, 1):
            for dt in (-1, 0, 1):
                if dg == 0 and dt == 0:
                    continue
                ok = (g + dg >= 0) & (g + dg < levels) & (t + dt >= 0) & (t + dt < tiles)
                if dg == 0:
                    ok = ok & (g == 0)

                @pl.when(ok)
                def _(dg=dg, dt=dt):
                    pl.semaphore_signal(barrier, inc=1, device_id=(g + dg, t + dt), device_id_type=MESH)

                count = count + ok.astype(jnp.int32)

    loads[0].wait()
    loads[1].wait()
    spread(qin, (), stage.at[0], 0)

    @pl.when(g == 0)
    def _():
        for step in range(STEPS):
            spread(nin, (step,), q.at[step], 8)

    for step in range(STEPS):
        @pl.when(jnp.logical_not(has_up))
        def _(step=step):
            q[step, :, 0:8, :] = jnp.zeros((4, 8, COLS), F32)

        @pl.when(jnp.logical_not(has_down))
        def _(step=step):
            q[step, :, 24:32, :] = jnp.zeros((4, 8, COLS), F32)

    def shift_copies(step):
        pairs = [
            (stage.at[step], q.at[step, :, 8:24, :], 0, not_last),
            (stage.at[step, :, 8:16, :], q.at[step, :, 0:8, :], 1, not_last & has_down),
            (stage.at[step, :, 0:8, :], q.at[step, :, 24:32, :], -1, not_last & has_up),
        ]
        return [
            (ok, pltpu.make_async_remote_copy(
                src_ref=src, dst_ref=dst, send_sem=send_sem.at[step, i], recv_sem=recv_sem.at[step, i],
                device_id=(g + 1, t + dt), device_id_type=MESH))
            for i, (src, dst, dt, ok) in enumerate(pairs)
        ]

    def noise_copies(step):
        pairs = [
            (q.at[step, :, 16:24, :], q.at[step, :, 0:8, :], 1, (g == 0) & has_down),
            (q.at[step, :, 8:16, :], q.at[step, :, 24:32, :], -1, (g == 0) & has_up),
        ]
        return [
            (ok, pltpu.make_async_remote_copy(
                src_ref=src, dst_ref=dst, send_sem=send_sem.at[step, 3 + i], recv_sem=recv_sem.at[step, 1 + i],
                device_id=(g, t + dt), device_id_type=MESH))
            for i, (src, dst, dt, ok) in enumerate(pairs)
        ]

    def term_copies(step):
        pairs = [
            (lo_send.at[step], hi_recv.at[step], -1, g > 0),
            (hi_send.at[step], lo_recv.at[step], 1, not_last),
        ]
        return [
            (ok, pltpu.make_async_remote_copy(
                src_ref=src, dst_ref=dst, send_sem=send_sem.at[step, 5 + i], recv_sem=recv_sem.at[step, 3 + i],
                device_id=(g + dg, t), device_id_type=MESH))
            for i, (src, dst, dg, ok) in enumerate(pairs)
        ]

    def start(copies):
        for ok, copy in copies:
            @pl.when(ok)
            def _(copy=copy):
                copy.start()

    def wait_send(copies):
        for ok, copy in copies:
            @pl.when(ok)
            def _(copy=copy):
                copy.wait_send()

    def wait_latents(step):
        copies = [copy for _, copy in shift_copies(step)]
        for copy, ok in zip(copies, (g > 0, has_up, has_down)):
            @pl.when(ok)
            def _(copy=copy):
                copy.wait_recv()

    def wait_terms(step):
        copies = [copy for _, copy in term_copies(step)]
        for copy, ok in zip(copies, (not_last, g > 0)):
            @pl.when(ok)
            def _(copy=copy):
                copy.wait_recv()

    if comm:
        pl.semaphore_wait(barrier, count)
        start(shift_copies(0))
        start(noise_copies(0))
        start(noise_copies(1))

    for step in range(STEPS):
        @pl.when(g == 0)
        def _(step=step):
            lo_recv[step] = jnp.zeros((16, COLS), F32)

        @pl.when(jnp.logical_not(not_last))
        def _(step=step):
            hi_recv[step] = jnp.zeros((16, COLS), F32)

    for slot in range(8):
        held[slot, CH:384, :] = jnp.zeros((64, 256), BF16)
    loads[2].wait()
    prepare_first(cf, w1t, w1, has_up.astype(F32), has_down.astype(F32))
    loads[3].wait()
    loads[4].wait()
    prepare_projection(op, tw, p16, pst)
    loads[5].wait()
    prepare_second(cs, wcat)

    for step in range(STEPS):
        now = q.at[step]
        if comm:
            wait_latents(step)
        window_columns(now, x1)
        for pair in range(2):
            for row in range(6):
                first_row(row, pair, x1, w1, stack)
            for row in range(4):
                second_row(row, pair, wcat, stack, pst, held, sums)
            if pair == 0:
                lo_send[step] = part(sums, 2, 0)
                hi_send[step] = part(sums, 1, 3)
                if comm:
                    start(term_copies(step))
        if comm:
            wait_terms(step)
        for frame in range(4):
            block = block_of(frame)
            before = lo_recv[step] if frame == 0 else part(sums, 1, frame - 1)
            after = hi_recv[step] if frame == 3 else part(sums, 2, frame + 1)
            projected = part(sums, 0, frame) + before + after
            fresh = keep[step, g, frame] * now[block, 8:24, :] - rate[step, g, frame] * projected
            stage[step + 1, block] = fresh.astype(BF16).astype(F32)
        if step + 1 < STEPS and comm:
            start(shift_copies(step + 1))

    for frame in range(4):
        for channel in range(4):
            out[frame, channel] = stage[STEPS, block_of(frame), pl.ds(channel, 4, stride=4), :].astype(BF16)

    if comm:
        for step in range(STEPS):
            wait_send(shift_copies(step))
            wait_send(noise_copies(step))
            wait_send(term_copies(step))


def call(levels, tiles, comm, *args):
    hbm = pl.BlockSpec(memory_space=pltpu.HBM)
    smem = pl.BlockSpec(memory_space=pltpu.SMEM)
    scratch = [
        pltpu.VMEM((4, 4, 4, COLS), BF16),
        pltpu.VMEM((2, 4, 4, 4, COLS), BF16),
        pltpu.VMEM((9, 4, CH), BF16),
        pltpu.VMEM((9, CH, CH), BF16),
        pltpu.VMEM((3, CH, CH), BF16),
        pltpu.VMEM((4, CH), BF16),
        pltpu.VMEM((CH, 9 * CH), BF16),
        pltpu.VMEM((COLS, 384), F32),
        pltpu.VMEM((6 * CH, COLS), BF16),
        pltpu.VMEM((16, CH), F32),
        pltpu.VMEM((2, 32, 704), F32),
        pltpu.VMEM((STEPS, 4, 32, COLS), F32),
        pltpu.VMEM((STEPS + 1, 4, 16, COLS), F32),
        pltpu.VMEM((96, 512), BF16),
        pltpu.VMEM((2, 18 * CH, 256), BF16),
        pltpu.VMEM((8, 704, 256), BF16),
        pltpu.VMEM((2, 3, 16, 256), F32),
        pltpu.VMEM((STEPS, 16, COLS), F32),
        pltpu.VMEM((STEPS, 16, COLS), F32),
        pltpu.VMEM((STEPS, 16, COLS), F32),
        pltpu.VMEM((STEPS, 16, COLS), F32),
        pltpu.SemaphoreType.DMA((6,)),
        pltpu.SemaphoreType.DMA((STEPS, 7)),
        pltpu.SemaphoreType.DMA((STEPS, 5)),
    ]
    return pl.pallas_call(
        functools.partial(kernel, levels, tiles, comm),
        out_shape=jax.ShapeDtypeStruct((4, 4, 4, COLS), BF16),
        in_specs=[hbm] * 6 + [smem] * 2,
        out_specs=pl.BlockSpec(memory_space=pltpu.VMEM),
        scratch_shapes=scratch,
        compiler_params=pltpu.CompilerParams(
            vmem_limit_bytes=62 << 20,
            **(dict(collective_id=0, has_side_effects=True) if comm else {}),
        ),
        name="queue_steps",
    )(*args)


def per_device(levels, tiles, queue_init, noise_frames, conv_first, conv_second, time_weight, out_proj, keep_coef, noise_coef):
    out = call(
        levels, tiles, True, queue_init[0], noise_frames, jnp.transpose(conv_first, (0, 1, 3, 2)).reshape(9, 4, CH), conv_second.reshape(9, CH, CH),
        time_weight, out_proj, keep_coef, noise_coef,
    )
    return out[None]


def solution(mesh):
    return jax.shard_map(
        functools.partial(per_device, mesh.shape["level"], mesh.shape["tile"]),
        mesh=mesh,
        in_specs=(
            P("level", None, None, "tile", None),
            P(None, None, None, "tile", None),
            P(),
            P(),
            P(),
            P(),
            P(),
            P(),
        ),
        out_specs=P("level", None, None, "tile", None),
        check_vma=False,
    )
```

```python
import functools

import jax
import jax.numpy as jnp
from jax import lax
from jax.experimental import pallas as pl
from jax.experimental.pallas import tpu as pltpu
from jax.sharding import PartitionSpec as P

STEPS = 2
CH = 320
COLS = 128
ORDER = (0, 3, 1, 2)
F32 = jnp.float32
BF16 = jnp.bfloat16
MESH = pl.DeviceIdType.MESH


def block_of(frame):
    return ORDER.index(frame)


def shifted_cols(value, amount):
    lane = lax.broadcasted_iota(jnp.int32, value.shape, 1)
    rolled = pltpu.roll(value, amount % COLS, 1)
    edge = 0 if amount == 1 else COLS - 1
    return jnp.where(lane == edge, jnp.zeros_like(rolled), rolled)


def spread(source, index, target):
    for frame in range(4):
        for channel in range(4):
            piece = source[index + (frame, channel)].astype(F32)
            target[block_of(frame), pl.ds(channel, 4, stride=4), :] = piece


def prepare_first(cf, w1t, w1, top_mask, bottom_mask):
    w1t[...] = jnp.zeros_like(w1t)
    for row_tap in range(3):
        for col_tap in range(3):
            place = col_tap * 32 + row_tap * 4
            w1t[place : place + 4, 0:CH] = cf[row_tap * 3 + col_tap].astype(F32) * 0.5
    base = jnp.transpose(w1t[...])[0:CH]
    for row in range(6):
        value = pltpu.roll(base, 4 * row, 1) if row else base
        if row == 0:
            value = value * top_mask
        if row == 5:
            value = value * bottom_mask
        w1[row * CH : (row + 1) * CH, :] = value.astype(BF16)


def prepare_second(cs, wt):
    for col_tap in range(3):
        lanes = slice(col_tap * CH, (col_tap + 1) * CH)
        g0, g1, g2 = (cs[a * 3 + col_tap].astype(F32) for a in range(3))
        outer = 0.25 * (g0 + g2)
        wt[0, :, lanes] = (0.5 * g0).astype(BF16)
        wt[1, :, lanes] = (outer + 0.25 * g1).astype(BF16)
        wt[2, :, lanes] = (outer - 0.25 * g1).astype(BF16)
        wt[3, :, lanes] = (0.5 * g2).astype(BF16)


def prepare_projection(op, tw, p16, pst):
    p16[...] = jnp.zeros_like(p16)
    p16[0:4, :] = op[...].astype(F32)
    p16[12:16, :] = op[...].astype(F32)
    both = p16[...].astype(BF16)
    pst[...] = jnp.zeros_like(pst)
    through = [jnp.dot(both, tw[k], preferred_element_type=F32) for k in range(3)]
    for odd in range(2):
        rows = slice(odd * 8, odd * 8 + 8)
        pst[odd, 0:8, 0:CH] = p16[rows, :] * 2.0
        for place, k in enumerate((1, 0, 2)):
            pst[odd, place * 8 : place * 8 + 8, 384 : 384 + CH] = through[k][rows]


def window_columns(half, q, x1):
    for block in range(4):
        lanes = slice(block * COLS, (block + 1) * COLS)
        if half == 0:
            value = jnp.concatenate([q[block, 0:24, :], jnp.zeros((8, COLS), F32)], axis=0)
        else:
            value = jnp.concatenate([jnp.zeros((8, COLS), F32), q[block, 8:32, :]], axis=0)
        x1[half, 0:32, lanes] = shifted_cols(value, 1).astype(BF16)
        x1[half, 32:64, lanes] = value.astype(BF16)
        x1[half, 64:96, lanes] = shifted_cols(value, -1).astype(BF16)


def first_row(row, half, pair, x1, w1, act):
    part = jnp.dot(
        w1[row * CH : (row + 1) * CH, 0:96], x1[half, :, pair * 256 : pair * 256 + 256], preferred_element_type=F32
    )
    act[pair, row] = (part + part * jnp.tanh(part)).astype(BF16)


def transform(half, pair, j, act, ust):
    left, right = ((0, 2), (1, 2), (2, 1), (1, 3))[j]
    for block in range(2):
        lanes = slice(block * COLS, (block + 1) * COLS)
        one = act[pair, 2 * half + left, :, lanes]
        two = act[pair, 2 * half + right, :, lanes]
        piece = one + two if j == 1 else one - two
        ust[half, pair, j, 0:CH, lanes] = shifted_cols(piece, 1)
        ust[half, pair, j, CH : 2 * CH, lanes] = piece
        ust[half, pair, j, 2 * CH : 3 * CH, lanes] = shifted_cols(piece, -1)


def product(half, pair, j, wt, ust, products):
    products[half, pair, j] = jnp.dot(wt[j], ust[half, pair, j], preferred_element_type=F32)


def second_rows(half, pair, products, held):
    for odd in range(2):
        one, two = products[half, pair, 1], products[half, pair, 2]
        value = products[half, pair, 0] + one + two if odd == 0 else one - two - products[half, pair, 3]
        held[half, pair, odd, 0:CH, :] = value.astype(BF16)
        held[half, pair, odd, 384 : 384 + CH, :] = (value + value * jnp.tanh(value)).astype(BF16)


def term_rows(half, pair, pst, held, sums):
    terms = [
        jnp.dot(pst[odd].astype(BF16), held[half, pair, odd], preferred_element_type=F32) for odd in range(2)
    ]
    total = terms[0] + terms[1]
    for place in range(3):
        sums[half, pair, place] = total[place * 8 : place * 8 + 8]


def part_of(sums, half, place, frame):
    block = block_of(frame)
    return sums[half, block // 2, place, :, (block % 2) * COLS : (block % 2 + 1) * COLS]


def kernel(levels, tiles, comm, queue_hbm, noise_hbm, cf_hbm, cs_hbm, tw_hbm, op_hbm, keep, rate, out,
           qin, nin, cf, cs, tw, op, wt, w1t, w1, p16, pst, q, stage, noise, zeros, x1, act, ust, products, held, sums,
           lo_send, hi_send, lo_recv, hi_recv, load_sem, send_sem, recv_sem, term_send_sem, term_recv_sem):
    if comm:
        g, t = lax.axis_index("level"), lax.axis_index("tile")
    else:
        g, t = jnp.int32(0), jnp.int32(1)
    has_up, has_down = t > 0, t < tiles - 1
    first_level, not_last = g == 0, g < levels - 1

    loads = [
        pltpu.make_async_copy(source, target, load_sem.at[i])
        for i, (source, target) in enumerate(
            [(queue_hbm, qin), (noise_hbm, nin), (cf_hbm, cf), (op_hbm, op), (tw_hbm, tw), (cs_hbm, cs)]
        )
    ]
    for load in loads:
        load.start()

    if comm:
        barrier = pltpu.get_barrier_semaphore()
        count = jnp.int32(0)
        for dg in (-1, 0, 1):
            for dt in (-1, 0, 1):
                if dg == 0 and dt == 0:
                    continue
                ok = (t + dt >= 0) & (t + dt < tiles)
                if dg == 0:
                    ok = ok & first_level

                @pl.when(ok)
                def _(dg=dg, dt=dt):
                    pl.semaphore_signal(
                        barrier, inc=1, device_id=(lax.rem(g + dg + levels, levels), t + dt), device_id_type=MESH
                    )

                count = count + ok.astype(jnp.int32)

    loads[0].wait()
    loads[1].wait()
    spread(qin, (), stage.at[0])
    for step in range(STEPS):
        spread(nin, (step,), noise.at[step])
    zeros[...] = jnp.zeros_like(zeros)

    def place(step, kind):
        start = (8, 16, 0, 24)[kind]
        return q.at[step, :, start : start + 8, :]

    def remote(source, step, kind, level, tile, send):
        return pltpu.make_async_remote_copy(
            src_ref=source, dst_ref=place(step, kind), send_sem=send_sem.at[step, send],
            recv_sem=recv_sem.at[step, kind], device_id=(level, tile), device_id_type=MESH,
        )

    def main_copy(step, half):
        return remote(stage.at[step, :, 8 * half : 8 * half + 8, :], step, half, g + 1, t, half)

    def halo_copy(step, half):
        source = stage.at[step, :, 8 * half : 8 * half + 8, :]
        return remote(source, step, 3 - half, g + 1, t + (1 if half else -1), 2 + half)

    def noise_copy(step, half):
        source = noise.at[step, :, 8 * half : 8 * half + 8, :]
        return remote(source, step, 3 - half, g, t + (1 if half else -1), 4 + half)

    def local_copy(source, step, kind):
        return pltpu.make_async_copy(source, place(step, kind), recv_sem.at[step, kind])

    def term_copies(step, half):
        return [
            pltpu.make_async_remote_copy(
                src_ref=source.at[step, half], dst_ref=target.at[step, half], send_sem=term_send_sem.at[step, half, i],
                recv_sem=term_recv_sem.at[step, half, i], device_id=(lax.rem(g + dg, levels), t), device_id_type=MESH,
            )
            for i, (source, target, dg) in enumerate([(lo_send, hi_recv, levels - 1), (hi_send, lo_recv, 1)])
        ]

    def neighbour(half):
        return has_down if half else has_up

    def start_shift(step, half):
        @pl.when(not_last)
        def _():
            main_copy(step, half).start()

            @pl.when(neighbour(half))
            def _():
                halo_copy(step, half).start()

    def wait_latents(step, kind):
        local_copy(zeros, step, kind).wait()

    if comm:
        @pl.when(first_level)
        def _():
            for step in range(STEPS):
                for half in range(2):
                    local_copy(noise.at[step, :, 8 * half : 8 * half + 8, :], step, half).start()

        for half in range(2):
            @pl.when(jnp.logical_not(neighbour(half)))
            def _(half=half):
                for step in range(STEPS):
                    local_copy(zeros, step, 2 + half).start()

        pl.semaphore_wait(barrier, count)
        for half in (1, 0):
            start_shift(0, half)
        for half in (1, 0):
            @pl.when(first_level & neighbour(half))
            def _(half=half):
                for step in range(STEPS):
                    noise_copy(step, half).start()

    for half in range(2):
        for pair in range(2):
            for odd in range(2):
                held[half, pair, odd, CH:384, :] = jnp.zeros((64, 256), BF16)
    loads[2].wait()
    prepare_first(cf, w1t, w1, has_up.astype(F32), has_down.astype(F32))
    loads[3].wait()
    loads[4].wait()
    prepare_projection(op, tw, p16, pst)
    loads[5].wait()
    prepare_second(cs, wt)

    lo_mask, hi_mask = (g > 0).astype(F32), not_last.astype(F32)
    for step in range(STEPS):
        now = q.at[step]
        early = 1 - step % 2
        late = 1 - early

        def send_terms(half):
            lo_send[step, half] = part_of(sums, half, 2, 0)
            hi_send[step, half] = part_of(sums, half, 1, 3)
            if comm:
                for copy in term_copies(step, half):
                    copy.start()

        def finish(half):
            if comm:
                for copy in term_copies(step, half):
                    copy.wait_recv()
            rows = slice(8 * half, 8 * half + 8)
            for frame in range(4):
                block = block_of(frame)
                before = lo_recv[step, half] * lo_mask if frame == 0 else part_of(sums, half, 1, frame - 1)
                after = hi_recv[step, half] * hi_mask if frame == 3 else part_of(sums, half, 2, frame + 1)
                projected = part_of(sums, half, 0, frame) + before + after
                latent = now[block, 8 + 8 * half : 16 + 8 * half, :]
                fresh = keep[step, g, frame] * latent - rate[step, g, frame] * projected
                stage[step + 1, block, rows, :] = fresh.astype(BF16).astype(F32)
            if comm and step + 1 < STEPS:
                start_shift(step + 1, half)

        if comm:
            for kind in (0, 1, 2 + early):
                wait_latents(step, kind)
        def first(half, pair, rows):
            for row in rows:
                first_row(row, half, pair, x1, w1, act)

        def shape(half, pair, j):
            transform(half, pair, j, act, ust)

        window_columns(early, now, x1)
        low = 2 * early
        units = [(early, 0), (early, 1), (late, 0), (late, 1)]
        fresh_rows = (0, 1) if early else (4, 5)
        rows_of = [(low, low + 2, low + 1, low + 3)] * 2 + [fresh_rows] * 2
        first(early, 0, rows_of[0])
        shape(early, 0, 0)
        for u, (half, pair) in enumerate(units):
            for j in range(4):
                if j == 1 and u == 1:
                    if comm:
                        wait_latents(step, 2 + late)
                    window_columns(late, now, x1)
                if j in (1, 2) and u < 3:
                    rows = rows_of[u + 1]
                    first(*units[u + 1], rows[: len(rows) // 2] if j == 1 else rows[len(rows) // 2 :])
                product(half, pair, j, wt, ust, products)
                if j < 3:
                    shape(half, pair, j + 1)
                elif u < 3:
                    shape(*units[u + 1], 0)
                if j == 0 and u:
                    second_rows(*units[u - 1], products, held)
                if j == 2 and u:
                    term_rows(*units[u - 1], pst, held, sums)
                    if u in (1, 3):
                        send_terms(early if u == 1 else late)
        second_rows(*units[3], products, held)
        finish(early)
        term_rows(late, 1, pst, held, sums)
        finish(late)

    for frame in range(4):
        for channel in range(4):
            out[frame, channel] = stage[STEPS, block_of(frame), pl.ds(channel, 4, stride=4), :].astype(BF16)

    if comm:
        for step in range(STEPS):
            for half in range(2):
                for copy in term_copies(step, half):
                    copy.wait_send()

                @pl.when(not_last)
                def _(step=step, half=half):
                    main_copy(step, half).wait_send()

                    @pl.when(neighbour(half))
                    def _():
                        halo_copy(step, half).wait_send()

                @pl.when(first_level & neighbour(half))
                def _(step=step, half=half):
                    noise_copy(step, half).wait_send()


def call(levels, tiles, comm, *args):
    hbm = pl.BlockSpec(memory_space=pltpu.HBM)
    smem = pl.BlockSpec(memory_space=pltpu.SMEM)
    scratch = [
        pltpu.VMEM((4, 4, 4, COLS), BF16),
        pltpu.VMEM((2, 4, 4, 4, COLS), BF16),
        pltpu.VMEM((9, 4, CH), BF16),
        pltpu.VMEM((9, CH, CH), BF16),
        pltpu.VMEM((3, CH, CH), BF16),
        pltpu.VMEM((4, CH), BF16),
        pltpu.VMEM((4, CH, 3 * CH), BF16),
        pltpu.VMEM((COLS, 384), F32),
        pltpu.VMEM((6 * CH, COLS), BF16),
        pltpu.VMEM((16, CH), F32),
        pltpu.VMEM((2, 32, 704), F32),
        pltpu.VMEM((STEPS, 4, 32, COLS), F32),
        pltpu.VMEM((STEPS + 1, 4, 16, COLS), F32),
        pltpu.VMEM((STEPS, 4, 16, COLS), F32),
        pltpu.VMEM((4, 8, COLS), F32),
        pltpu.VMEM((2, 96, 512), BF16),
        pltpu.VMEM((2, 6, CH, 256), BF16),
        pltpu.VMEM((2, 2, 4, 3 * CH, 256), BF16),
        pltpu.VMEM((2, 2, 4, CH, 256), F32),
        pltpu.VMEM((2, 2, 2, 704, 256), BF16),
        pltpu.VMEM((2, 2, 3, 8, 256), F32),
        pltpu.VMEM((STEPS, 2, 8, COLS), F32),
        pltpu.VMEM((STEPS, 2, 8, COLS), F32),
        pltpu.VMEM((STEPS, 2, 8, COLS), F32),
        pltpu.VMEM((STEPS, 2, 8, COLS), F32),
        pltpu.SemaphoreType.DMA((6,)),
        pltpu.SemaphoreType.DMA((STEPS, 6)),
        pltpu.SemaphoreType.DMA((STEPS, 4)),
        pltpu.SemaphoreType.DMA((STEPS, 2, 2)),
        pltpu.SemaphoreType.DMA((STEPS, 2, 2)),
    ]
    return pl.pallas_call(
        functools.partial(kernel, levels, tiles, comm),
        out_shape=jax.ShapeDtypeStruct((4, 4, 4, COLS), BF16),
        in_specs=[hbm] * 6 + [smem] * 2,
        out_specs=pl.BlockSpec(memory_space=pltpu.VMEM),
        scratch_shapes=scratch,
        compiler_params=pltpu.CompilerParams(
            vmem_limit_bytes=62 << 20,
            **(dict(collective_id=0, has_side_effects=True) if comm else {}),
        ),
        name="queue_steps",
    )(*args)


def per_device(levels, tiles, queue_init, noise_frames, conv_first, conv_second, time_weight, out_proj, keep_coef, noise_coef):
    out = call(
        levels, tiles, True, queue_init[0], noise_frames, jnp.transpose(conv_first, (0, 1, 3, 2)).reshape(9, 4, CH), conv_second.reshape(9, CH, CH),
        time_weight, out_proj, keep_coef, noise_coef,
    )
    return out[None]


def solution(mesh):
    return jax.shard_map(
        functools.partial(per_device, mesh.shape["level"], mesh.shape["tile"]),
        mesh=mesh,
        in_specs=(
            P("level", None, None, "tile", None),
            P(None, None, None, "tile", None),
            P(),
            P(),
            P(),
            P(),
            P(),
            P(),
        ),
        out_specs=P("level", None, None, "tile", None),
        check_vma=False,
    )
```

```python
import functools

import jax
import jax.numpy as jnp
from jax import lax
from jax.experimental import pallas as pl
from jax.experimental.pallas import tpu as pltpu
from jax.sharding import PartitionSpec as P

STEPS = 2
CH = 320
COLS = 128
ORDER = (0, 3, 1, 2)
F32 = jnp.float32
BF16 = jnp.bfloat16
MESH = pl.DeviceIdType.MESH


def block_of(frame):
    return ORDER.index(frame)


def shifted_cols(value, amount):
    lane = lax.broadcasted_iota(jnp.int32, value.shape, 1)
    rolled = pltpu.roll(value, amount % COLS, 1)
    edge = 0 if amount == 1 else COLS - 1
    return jnp.where(lane == edge, jnp.zeros_like(rolled), rolled)


def spread(source, index, target):
    for frame in range(4):
        for channel in range(4):
            piece = source[index + (frame, channel)].astype(F32)
            target[block_of(frame), pl.ds(channel, 4, stride=4), :] = piece


def prepare_first(cf, w1t, w1, top_mask, bottom_mask):
    w1t[...] = jnp.zeros_like(w1t)
    for row_tap in range(3):
        for col_tap in range(3):
            place = col_tap * 32 + row_tap * 4
            w1t[place : place + 4, 0:CH] = cf[row_tap * 3 + col_tap].astype(F32) * 0.5
    base = jnp.transpose(w1t[...])[0:CH]
    for row in range(6):
        value = pltpu.roll(base, 4 * row, 1) if row else base
        if row == 0:
            value = value * top_mask
        if row == 5:
            value = value * bottom_mask
        w1[row * CH : (row + 1) * CH, :] = value.astype(BF16)


def prepare_second(cs, wt):
    for col_tap in range(3):
        lanes = slice(col_tap * CH, (col_tap + 1) * CH)
        g0, g1, g2 = (cs[a * 3 + col_tap].astype(F32) for a in range(3))
        outer = 0.25 * (g0 + g2)
        wt[0, :, lanes] = (0.5 * g0).astype(BF16)
        wt[1, :, lanes] = (outer + 0.25 * g1).astype(BF16)
        wt[2, :, lanes] = (outer - 0.25 * g1).astype(BF16)
        wt[3, :, lanes] = (0.5 * g2).astype(BF16)


def prepare_projection(op, tw, p16, pst):
    p16[...] = jnp.zeros_like(p16)
    p16[0:4, :] = op[...].astype(F32)
    p16[12:16, :] = op[...].astype(F32)
    both = p16[...].astype(BF16)
    pst[...] = jnp.zeros_like(pst)
    through = [jnp.dot(both, tw[k], preferred_element_type=F32) for k in range(3)]
    for odd in range(2):
        rows = slice(odd * 8, odd * 8 + 8)
        pst[odd, 0:8, 0:CH] = p16[rows, :] * 2.0
        for place, k in enumerate((1, 0, 2)):
            pst[odd, place * 8 : place * 8 + 8, 384 : 384 + CH] = through[k][rows]


def window_columns(half, q, x1):
    for block in range(4):
        lanes = slice(block * COLS, (block + 1) * COLS)
        if half == 0:
            value = jnp.concatenate([q[block, 0:24, :], jnp.zeros((8, COLS), F32)], axis=0)
        else:
            value = jnp.concatenate([jnp.zeros((8, COLS), F32), q[block, 8:32, :]], axis=0)
        x1[half, 0:32, lanes] = shifted_cols(value, 1).astype(BF16)
        x1[half, 32:64, lanes] = value.astype(BF16)
        x1[half, 64:96, lanes] = shifted_cols(value, -1).astype(BF16)


def first_row(row, half, pair, x1, w1, act):
    part = jnp.dot(
        w1[row * CH : (row + 1) * CH, 0:96], x1[half, :, pair * 256 : pair * 256 + 256], preferred_element_type=F32
    )
    act[pair, row] = (part + part * jnp.tanh(part)).astype(BF16)


def transform(half, pair, j, act, ust):
    left, right = ((0, 2), (1, 2), (2, 1), (1, 3))[j]
    for block in range(2):
        lanes = slice(block * COLS, (block + 1) * COLS)
        one = act[pair, 2 * half + left, :, lanes]
        two = act[pair, 2 * half + right, :, lanes]
        piece = one + two if j == 1 else one - two
        ust[half, pair, j, 0:CH, lanes] = shifted_cols(piece, 1)
        ust[half, pair, j, CH : 2 * CH, lanes] = piece
        ust[half, pair, j, 2 * CH : 3 * CH, lanes] = shifted_cols(piece, -1)


def product(half, pair, j, wt, ust, products):
    products[half, pair, j] = jnp.dot(wt[j], ust[half, pair, j], preferred_element_type=F32)


def second_rows(half, pair, products, held):
    for odd in range(2):
        one, two = products[half, pair, 1], products[half, pair, 2]
        value = products[half, pair, 0] + one + two if odd == 0 else one - two - products[half, pair, 3]
        held[half, pair, odd, 0:CH, :] = value.astype(BF16)
        held[half, pair, odd, 384 : 384 + CH, :] = (value + value * jnp.tanh(value)).astype(BF16)


def term_rows(half, pair, pst, held, sums):
    terms = [
        jnp.dot(pst[odd].astype(BF16), held[half, pair, odd], preferred_element_type=F32) for odd in range(2)
    ]
    total = terms[0] + terms[1]
    for place in range(3):
        sums[half, pair, place] = total[place * 8 : place * 8 + 8]


def part_of(sums, half, place, frame):
    block = block_of(frame)
    return sums[half, block // 2, place, :, (block % 2) * COLS : (block % 2 + 1) * COLS]


def kernel(levels, tiles, comm, queue_hbm, noise_hbm, cf_hbm, cs_hbm, tw_hbm, op_hbm, keep, rate, out,
           qin, nin, cf, cs, tw, op, wt, w1t, w1, p16, pst, q, stage, noise, zeros, x1, act, ust, products, held, sums,
           lo_send, hi_send, lo_recv, hi_recv, load_sem, send_sem, recv_sem, term_send_sem, term_recv_sem):
    if comm:
        g, t = lax.axis_index("level"), lax.axis_index("tile")
    else:
        g, t = jnp.int32(0), jnp.int32(1)
    has_up, has_down = t > 0, t < tiles - 1
    first_level, not_last = g == 0, g < levels - 1

    loads = [
        pltpu.make_async_copy(source, target, load_sem.at[i])
        for i, (source, target) in enumerate(
            [(queue_hbm, qin), (noise_hbm, nin), (cf_hbm, cf), (op_hbm, op), (tw_hbm, tw), (cs_hbm, cs)]
        )
    ]
    for load in loads:
        load.start()

    if comm:
        barrier = pltpu.get_barrier_semaphore()
        count = jnp.int32(0)
        for dg in (-1, 0, 1):
            for dt in (-1, 0, 1):
                if dg == 0 and dt == 0:
                    continue
                ok = (t + dt >= 0) & (t + dt < tiles)
                if dg == 0:
                    ok = ok & first_level

                @pl.when(ok)
                def _(dg=dg, dt=dt):
                    pl.semaphore_signal(
                        barrier, inc=1, device_id=(lax.rem(g + dg + levels, levels), t + dt), device_id_type=MESH
                    )

                count = count + ok.astype(jnp.int32)

    loads[0].wait()
    spread(qin, (), stage.at[0])
    zeros[...] = jnp.zeros_like(zeros)

    def place(step, kind):
        start = (8, 16, 0, 24)[kind]
        return q.at[step, :, start : start + 8, :]

    def remote(source, step, kind, level, tile, send):
        return pltpu.make_async_remote_copy(
            src_ref=source, dst_ref=place(step, kind), send_sem=send_sem.at[step, send],
            recv_sem=recv_sem.at[step, kind], device_id=(level, tile), device_id_type=MESH,
        )

    def main_copy(step, half):
        return remote(stage.at[step, :, 8 * half : 8 * half + 8, :], step, half, g + 1, t, half)

    def halo_copy(step, half):
        source = stage.at[step, :, 8 * half : 8 * half + 8, :]
        return remote(source, step, 3 - half, g + 1, t + (1 if half else -1), 2 + half)

    def noise_copy(step, half):
        source = noise.at[step, :, 8 * half : 8 * half + 8, :]
        return remote(source, step, 3 - half, g, t + (1 if half else -1), 4 + half)

    def local_copy(source, step, kind):
        return pltpu.make_async_copy(source, place(step, kind), recv_sem.at[step, kind])

    def term_copies(step, half):
        return [
            pltpu.make_async_remote_copy(
                src_ref=source.at[step, half], dst_ref=target.at[step, half], send_sem=term_send_sem.at[step, half, i],
                recv_sem=term_recv_sem.at[step, half, i], device_id=(lax.rem(g + dg, levels), t), device_id_type=MESH,
            )
            for i, (source, target, dg) in enumerate([(lo_send, hi_recv, levels - 1), (hi_send, lo_recv, 1)])
        ]

    def neighbour(half):
        return has_down if half else has_up

    def start_shift(step, half):
        @pl.when(not_last)
        def _():
            main_copy(step, half).start()

            @pl.when(neighbour(half))
            def _():
                halo_copy(step, half).start()

    def wait_latents(step, kind):
        local_copy(zeros, step, kind).wait()

    if comm:
        pl.semaphore_wait(barrier, count)
        for half in (1, 0):
            start_shift(0, half)
        loads[1].wait()

        @pl.when(first_level)
        def _():
            for step in range(STEPS):
                spread(nin, (step,), noise.at[step])
                for half in range(2):
                    local_copy(noise.at[step, :, 8 * half : 8 * half + 8, :], step, half).start()

        for half in range(2):
            @pl.when(jnp.logical_not(neighbour(half)))
            def _(half=half):
                for step in range(STEPS):
                    local_copy(zeros, step, 2 + half).start()

        for half in (1, 0):
            @pl.when(first_level & neighbour(half))
            def _(half=half):
                for step in range(STEPS):
                    noise_copy(step, half).start()

    if not comm:
        loads[1].wait()
    for half in range(2):
        for pair in range(2):
            for odd in range(2):
                held[half, pair, odd, CH:384, :] = jnp.zeros((64, 256), BF16)
    loads[2].wait()
    prepare_first(cf, w1t, w1, has_up.astype(F32), has_down.astype(F32))
    loads[3].wait()
    loads[4].wait()
    prepare_projection(op, tw, p16, pst)
    loads[5].wait()
    prepare_second(cs, wt)

    lo_mask, hi_mask = (g > 0).astype(F32), not_last.astype(F32)
    for step in range(STEPS):
        now = q.at[step]
        early = step % 2
        late = 1 - early

        def send_terms(half):
            lo_send[step, half] = part_of(sums, half, 2, 0)
            hi_send[step, half] = part_of(sums, half, 1, 3)
            if comm:
                for copy in term_copies(step, half):
                    copy.start()

        def finish(half):
            if comm:
                for copy in term_copies(step, half):
                    copy.wait_recv()
            rows = slice(8 * half, 8 * half + 8)
            for frame in range(4):
                block = block_of(frame)
                before = lo_recv[step, half] * lo_mask if frame == 0 else part_of(sums, half, 1, frame - 1)
                after = hi_recv[step, half] * hi_mask if frame == 3 else part_of(sums, half, 2, frame + 1)
                projected = part_of(sums, half, 0, frame) + before + after
                latent = now[block, 8 + 8 * half : 16 + 8 * half, :]
                fresh = keep[step, g, frame] * latent - rate[step, g, frame] * projected
                stage[step + 1, block, rows, :] = fresh.astype(BF16).astype(F32)
            if comm and step + 1 < STEPS:
                start_shift(step + 1, half)

        if comm:
            for kind in (0, 1, 2 + early):
                wait_latents(step, kind)
        def first(half, pair, rows):
            for row in rows:
                first_row(row, half, pair, x1, w1, act)

        def shape(half, pair, j):
            transform(half, pair, j, act, ust)

        window_columns(early, now, x1)
        low = 2 * early
        units = [(early, 0), (early, 1), (late, 0), (late, 1)]
        fresh_rows = (0, 1) if early else (4, 5)
        rows_of = [fresh_rows if half == late else (low, low + 2, low + 1, low + 3) for half, _ in units]
        windowed = [early]
        first(early, 0, rows_of[0])
        shape(early, 0, 0)
        for u, (half, pair) in enumerate(units):
            for j in range(4):
                if j in (1, 2) and u < 3:
                    if units[u + 1][0] not in windowed:
                        if comm:
                            wait_latents(step, 2 + late)
                        window_columns(late, now, x1)
                        windowed.append(late)
                    rows = rows_of[u + 1]
                    first(*units[u + 1], rows[: len(rows) // 2] if j == 1 else rows[len(rows) // 2 :])
                product(half, pair, j, wt, ust, products)
                if j < 3:
                    shape(half, pair, j + 1)
                elif u < 3:
                    shape(*units[u + 1], 0)
                if j == 0 and u:
                    second_rows(*units[u - 1], products, held)
                if j == 1 and u:
                    term_rows(*units[u - 1], pst, held, sums)
                    if units[u - 1][1] == 0:
                        send_terms(units[u - 1][0])
                if u == 3 and j == 3:
                    finish(early)
        second_rows(*units[3], products, held)
        term_rows(*units[3], pst, held, sums)
        finish(late)

    for frame in range(4):
        for channel in range(4):
            out[frame, channel] = stage[STEPS, block_of(frame), pl.ds(channel, 4, stride=4), :].astype(BF16)

    if comm:
        for step in range(STEPS):
            for half in range(2):
                for copy in term_copies(step, half):
                    copy.wait_send()

                @pl.when(not_last)
                def _(step=step, half=half):
                    main_copy(step, half).wait_send()

                    @pl.when(neighbour(half))
                    def _():
                        halo_copy(step, half).wait_send()

                @pl.when(first_level & neighbour(half))
                def _(step=step, half=half):
                    noise_copy(step, half).wait_send()


def call(levels, tiles, comm, *args):
    hbm = pl.BlockSpec(memory_space=pltpu.HBM)
    smem = pl.BlockSpec(memory_space=pltpu.SMEM)
    scratch = [
        pltpu.VMEM((4, 4, 4, COLS), BF16),
        pltpu.VMEM((2, 4, 4, 4, COLS), BF16),
        pltpu.VMEM((9, 4, CH), BF16),
        pltpu.VMEM((9, CH, CH), BF16),
        pltpu.VMEM((3, CH, CH), BF16),
        pltpu.VMEM((4, CH), BF16),
        pltpu.VMEM((4, CH, 3 * CH), BF16),
        pltpu.VMEM((COLS, 384), F32),
        pltpu.VMEM((6 * CH, COLS), BF16),
        pltpu.VMEM((16, CH), F32),
        pltpu.VMEM((2, 32, 704), F32),
        pltpu.VMEM((STEPS, 4, 32, COLS), F32),
        pltpu.VMEM((STEPS + 1, 4, 16, COLS), F32),
        pltpu.VMEM((STEPS, 4, 16, COLS), F32),
        pltpu.VMEM((4, 8, COLS), F32),
        pltpu.VMEM((2, 96, 512), BF16),
        pltpu.VMEM((2, 6, CH, 256), BF16),
        pltpu.VMEM((2, 2, 4, 3 * CH, 256), BF16),
        pltpu.VMEM((2, 2, 4, CH, 256), F32),
        pltpu.VMEM((2, 2, 2, 704, 256), BF16),
        pltpu.VMEM((2, 2, 3, 8, 256), F32),
        pltpu.VMEM((STEPS, 2, 8, COLS), F32),
        pltpu.VMEM((STEPS, 2, 8, COLS), F32),
        pltpu.VMEM((STEPS, 2, 8, COLS), F32),
        pltpu.VMEM((STEPS, 2, 8, COLS), F32),
        pltpu.SemaphoreType.DMA((6,)),
        pltpu.SemaphoreType.DMA((STEPS, 6)),
        pltpu.SemaphoreType.DMA((STEPS, 4)),
        pltpu.SemaphoreType.DMA((STEPS, 2, 2)),
        pltpu.SemaphoreType.DMA((STEPS, 2, 2)),
    ]
    return pl.pallas_call(
        functools.partial(kernel, levels, tiles, comm),
        out_shape=jax.ShapeDtypeStruct((4, 4, 4, COLS), BF16),
        in_specs=[hbm] * 6 + [smem] * 2,
        out_specs=pl.BlockSpec(memory_space=pltpu.VMEM),
        scratch_shapes=scratch,
        compiler_params=pltpu.CompilerParams(
            vmem_limit_bytes=62 << 20,
            **(dict(collective_id=0, has_side_effects=True) if comm else {}),
        ),
        name="queue_steps",
    )(*args)


def per_device(levels, tiles, queue_init, noise_frames, conv_first, conv_second, time_weight, out_proj, keep_coef, noise_coef):
    out = call(
        levels, tiles, True, queue_init[0], noise_frames, jnp.transpose(conv_first, (0, 1, 3, 2)).reshape(9, 4, CH), conv_second.reshape(9, CH, CH),
        time_weight, out_proj, keep_coef, noise_coef,
    )
    return out[None]


def solution(mesh):
    return jax.shard_map(
        functools.partial(per_device, mesh.shape["level"], mesh.shape["tile"]),
        mesh=mesh,
        in_specs=(
            P("level", None, None, "tile", None),
            P(None, None, None, "tile", None),
            P(),
            P(),
            P(),
            P(),
            P(),
            P(),
        ),
        out_specs=P("level", None, None, "tile", None),
        check_vma=False,
    )
```

```python
import functools

import jax
import jax.numpy as jnp
from jax import lax
from jax.experimental import pallas as pl
from jax.experimental.pallas import tpu as pltpu
from jax.sharding import PartitionSpec as P

STEPS = 2
CH = 320
COLS = 128
ORDER = (0, 3, 1, 2)
F32 = jnp.float32
BF16 = jnp.bfloat16
MESH = pl.DeviceIdType.MESH


def block_of(frame):
    return ORDER.index(frame)


def shifted_cols(value, amount):
    lane = lax.broadcasted_iota(jnp.int32, value.shape, 1)
    rolled = pltpu.roll(value, amount % COLS, 1)
    edge = 0 if amount == 1 else COLS - 1
    return jnp.where(lane == edge, jnp.zeros_like(rolled), rolled)


def spread(source, index, target):
    for frame in range(4):
        for channel in range(4):
            piece = source[index + (frame, channel)].astype(F32)
            target[block_of(frame), pl.ds(channel, 4, stride=4), :] = piece


def prepare_first(cf, w1t, w1, top_mask, bottom_mask):
    w1t[...] = jnp.zeros_like(w1t)
    for row_tap in range(3):
        for col_tap in range(3):
            place = col_tap * 32 + row_tap * 4
            w1t[place : place + 4, 0:CH] = cf[row_tap * 3 + col_tap].astype(F32) * 0.5
    base = jnp.transpose(w1t[...])[0:CH]
    for row in range(6):
        value = pltpu.roll(base, 4 * row, 1) if row else base
        if row == 0:
            value = value * top_mask
        if row == 5:
            value = value * bottom_mask
        w1[row * CH : (row + 1) * CH, :] = value.astype(BF16)


def prepare_second(cs, wt):
    for col_tap in range(3):
        lanes = slice(col_tap * CH, (col_tap + 1) * CH)
        g0, g1, g2 = (cs[a * 3 + col_tap].astype(F32) for a in range(3))
        outer = 0.25 * (g0 + g2)
        wt[0, :, lanes] = (0.5 * g0).astype(BF16)
        wt[1, :, lanes] = (outer + 0.25 * g1).astype(BF16)
        wt[2, :, lanes] = (outer - 0.25 * g1).astype(BF16)
        wt[3, :, lanes] = (0.5 * g2).astype(BF16)


def prepare_projection(op, tw, p16, pst):
    p16[...] = jnp.zeros_like(p16)
    p16[0:4, :] = op[...].astype(F32)
    p16[12:16, :] = op[...].astype(F32)
    both = p16[...].astype(BF16)
    pst[...] = jnp.zeros_like(pst)
    through = [jnp.dot(both, tw[k], preferred_element_type=F32) for k in range(3)]
    for odd in range(2):
        rows = slice(odd * 8, odd * 8 + 8)
        pst[odd, 0:8, 0:CH] = p16[rows, :] * 2.0
        for place, k in enumerate((1, 0, 2)):
            pst[odd, place * 8 : place * 8 + 8, 384 : 384 + CH] = through[k][rows]


def window_columns(half, q, x1, far=None):
    for block in range(4):
        lanes = slice(block * COLS, (block + 1) * COLS)
        if far is not None:
            value = jnp.concatenate([far[block], q[block, 0:16, :], jnp.zeros((8, COLS), F32)], axis=0)
        elif half == 0:
            value = jnp.concatenate([q[block, 0:24, :], jnp.zeros((8, COLS), F32)], axis=0)
        else:
            value = jnp.concatenate([jnp.zeros((8, COLS), F32), q[block, 8:32, :]], axis=0)
        x1[half, 0:32, lanes] = shifted_cols(value, 1).astype(BF16)
        x1[half, 32:64, lanes] = value.astype(BF16)
        x1[half, 64:96, lanes] = shifted_cols(value, -1).astype(BF16)


def first_row(row, half, pair, x1, w1, act):
    part = jnp.dot(
        w1[row * CH : (row + 1) * CH, 0:96], x1[half, :, pair * 256 : pair * 256 + 256], preferred_element_type=F32
    )
    act[pair, row] = (part + part * jnp.tanh(part)).astype(BF16)


def transform(half, pair, j, act, ust):
    left, right = ((0, 2), (1, 2), (2, 1), (1, 3))[j]
    for block in range(2):
        lanes = slice(block * COLS, (block + 1) * COLS)
        one = act[pair, 2 * half + left, :, lanes]
        two = act[pair, 2 * half + right, :, lanes]
        piece = one + two if j == 1 else one - two
        ust[half, pair, j, 0:CH, lanes] = shifted_cols(piece, 1)
        ust[half, pair, j, CH : 2 * CH, lanes] = piece
        ust[half, pair, j, 2 * CH : 3 * CH, lanes] = shifted_cols(piece, -1)


def product(half, pair, j, wt, ust, products):
    products[half, pair, j] = jnp.dot(wt[j], ust[half, pair, j], preferred_element_type=F32)


def second_rows(half, pair, products, held, slot=None):
    slot = half if slot is None else slot
    for odd in range(2):
        one, two = products[half, pair, 1], products[half, pair, 2]
        value = products[half, pair, 0] + one + two if odd == 0 else one - two - products[half, pair, 3]
        held[slot, pair, odd, 0:CH, :] = value.astype(BF16)
        held[slot, pair, odd, 384 : 384 + CH, :] = (value + value * jnp.tanh(value)).astype(BF16)


def term_rows(half, pair, pst, held, sums):
    terms = [
        jnp.dot(pst[odd].astype(BF16), held[half, pair, odd], preferred_element_type=F32) for odd in range(2)
    ]
    total = terms[0] + terms[1]
    for place in range(3):
        sums[half, pair, place] = total[place * 8 : place * 8 + 8]


def part_of(sums, half, place, frame):
    block = block_of(frame)
    return sums[half, block // 2, place, :, (block % 2) * COLS : (block % 2 + 1) * COLS]


def kernel(levels, tiles, comm, queue_hbm, noise_hbm, cf_hbm, cs_hbm, tw_hbm, op_hbm, keep, rate, out,
           qin, nin, cf, cs, tw, op, wt, w1t, w1, p16, pst, q, stage, noise, zeros, x1, act, ust, products, held, sums,
           lo_send, hi_send, lo_recv, hi_recv, load_sem, send_sem, recv_sem, term_send_sem, term_recv_sem,
           far_ready, far, border, far_send_sem, far_recv_sem):
    if comm:
        g, t = lax.axis_index("level"), lax.axis_index("tile")
    else:
        g, t = jnp.int32(0), jnp.int32(1)
    has_up, has_down = t > 0, t < tiles - 1
    first_level, not_last = g == 0, g < levels - 1
    period = max(tiles // 4, 1)
    edge = has_up & (lax.rem(t, period) == 0)
    next_edge = has_down & (lax.rem(t + 1, period) == 0)
    redo, next_redo = edge, next_edge

    loads = [
        pltpu.make_async_copy(source, target, load_sem.at[i])
        for i, (source, target) in enumerate(
            [(queue_hbm, qin), (noise_hbm, nin), (cf_hbm, cf), (op_hbm, op), (tw_hbm, tw), (cs_hbm, cs)]
        )
    ]
    for load in loads:
        load.start()

    if comm:
        barrier = pltpu.get_barrier_semaphore()
        count = jnp.int32(0)
        for dg in (-1, 0, 1):
            for dt in (-1, 0, 1):
                if dg == 0 and dt == 0:
                    continue
                ok = (t + dt >= 0) & (t + dt < tiles)
                if dg == 0:
                    ok = ok & first_level

                @pl.when(ok & jnp.logical_not(next_edge) if dt == 1 else ok)
                def _(dg=dg, dt=dt):
                    pl.semaphore_signal(
                        barrier, inc=1, device_id=(lax.rem(g + dg + levels, levels), t + dt), device_id_type=MESH
                    )

                counted = ok & jnp.logical_not(edge) if dt == -1 else ok
                count = count + counted.astype(jnp.int32)

    loads[0].wait()
    spread(qin, (), stage.at[0])
    zeros[...] = jnp.zeros_like(zeros)

    def place(step, kind):
        start = (8, 16, 0, 24)[kind]
        return q.at[step, :, start : start + 8, :]

    def remote(source, step, kind, level, tile, send):
        return pltpu.make_async_remote_copy(
            src_ref=source, dst_ref=place(step, kind), send_sem=send_sem.at[step, send],
            recv_sem=recv_sem.at[step, kind], device_id=(level, tile), device_id_type=MESH,
        )

    def main_copy(step, half):
        return remote(stage.at[step, :, 8 * half : 8 * half + 8, :], step, half, g + 1, t, half)

    def halo_copy(step, half):
        source = stage.at[step, :, 8 * half : 8 * half + 8, :]
        return remote(source, step, 3 - half, g + 1, t + (1 if half else -1), 2 + half)

    def noise_copy(step, half):
        source = noise.at[step, :, 8 * half : 8 * half + 8, :]
        return remote(source, step, 3 - half, g, t + (1 if half else -1), 4 + half)

    def local_copy(source, step, kind):
        return pltpu.make_async_copy(source, place(step, kind), recv_sem.at[step, kind])

    def term_copies(step, half):
        return [
            pltpu.make_async_remote_copy(
                src_ref=source.at[step, half], dst_ref=target.at[step, half], send_sem=term_send_sem.at[step, half, i],
                recv_sem=term_recv_sem.at[step, half, i], device_id=(lax.rem(g + dg, levels), t), device_id_type=MESH,
            )
            for i, (source, target, dg) in enumerate([(lo_send, hi_recv, levels - 1), (hi_send, lo_recv, 1)])
        ]

    def neighbour(half, step=0):
        if half and step:
            return has_down & jnp.logical_not(next_redo)
        return has_down if half else has_up

    def far_copy(source, level, send):
        return pltpu.make_async_remote_copy(
            src_ref=source, dst_ref=far, send_sem=far_send_sem.at[send], recv_sem=far_recv_sem,
            device_id=(level, t + 1), device_id_type=MESH,
        )

    def far_copies():
        return [
            (next_redo & not_last, far_copy(stage.at[0, :, 0:8, :], g + 1, 0)),
            (next_redo & first_level, far_copy(noise.at[0, :, 0:8, :], 0 * g, 1)),
        ]

    def border_copy():
        return pltpu.make_async_remote_copy(
            src_ref=border, dst_ref=place(1, 2), send_sem=far_send_sem.at[2], recv_sem=recv_sem.at[1, 2],
            device_id=(g + 1, t), device_id_type=MESH,
        )

    def start_shift(step, half):
        @pl.when(not_last)
        def _():
            main_copy(step, half).start()

            @pl.when(neighbour(half) & jnp.logical_not(edge) if step == 0 and half == 0 else neighbour(half, step))
            def _():
                halo_copy(step, half).start()

    def far_sends():
        pl.semaphore_wait(far_ready, 2 + first_level.astype(jnp.int32))

        @pl.when(not_last)
        def _():
            halo_copy(0, 0).start()

        @pl.when(first_level)
        def _():
            for step in range(STEPS):
                noise_copy(step, 0).start()

    def wait_latents(step, kind):
        local_copy(zeros, step, kind).wait()

    if comm:
        pl.semaphore_wait(barrier, count)
        for dg in (-1, 0, 1):
            @pl.when(next_edge & first_level if dg == 0 else next_edge)
            def _(dg=dg):
                pl.semaphore_signal(
                    far_ready, inc=1, device_id=(lax.rem(g + dg + levels, levels), t + 1), device_id_type=MESH
                )

        for half in (1, 0):
            start_shift(0, half)
        loads[1].wait()

        @pl.when(first_level)
        def _():
            for step in range(STEPS):
                spread(nin, (step,), noise.at[step])
                for half in range(2):
                    local_copy(noise.at[step, :, 8 * half : 8 * half + 8, :], step, half).start()

        for half in range(2):
            @pl.when(jnp.logical_not(neighbour(half)))
            def _(half=half):
                for step in range(STEPS):
                    local_copy(zeros, step, 2 + half).start()

        for half in (1, 0):
            @pl.when(first_level & neighbour(half) & (jnp.logical_not(edge) if half == 0 else has_down))
            def _(half=half):
                for step in range(STEPS):
                    noise_copy(step, half).start()

        for ok, copy in far_copies():
            @pl.when(ok)
            def _(copy=copy):
                copy.start()

    if not comm:
        loads[1].wait()
    for half in range(3):
        for pair in range(2):
            for odd in range(2):
                held[half, pair, odd, CH:384, :] = jnp.zeros((64, 256), BF16)
    loads[2].wait()
    prepare_first(cf, w1t, w1, has_up.astype(F32), has_down.astype(F32))
    loads[3].wait()
    loads[4].wait()
    prepare_projection(op, tw, p16, pst)
    loads[5].wait()
    prepare_second(cs, wt)

    lo_mask, hi_mask = (g > 0).astype(F32), not_last.astype(F32)
    def run(step, early, far_tile):
        now = q.at[step]
        late = 1 - early

        def send_terms(half):
            lo_send[step, half] = part_of(sums, half, 2, 0)
            hi_send[step, half] = part_of(sums, half, 1, 3)
            if comm:
                for copy in term_copies(step, half):
                    copy.start()

        def finish(half):
            if comm:
                for copy in term_copies(step, half):
                    copy.wait_recv()
            rows = slice(8 * half, 8 * half + 8)
            for frame in range(4):
                block = block_of(frame)
                before = lo_recv[step, half] * lo_mask if frame == 0 else part_of(sums, half, 1, frame - 1)
                after = hi_recv[step, half] * hi_mask if frame == 3 else part_of(sums, half, 2, frame + 1)
                projected = part_of(sums, half, 0, frame) + before + after
                latent = now[block, 0:8, :] if half == 2 else now[block, 8 + 8 * half : 16 + 8 * half, :]
                fresh = keep[step, g, frame] * latent - rate[step, g, frame] * projected
                fresh = fresh.astype(BF16).astype(F32)
                if half == 2:
                    border[block] = fresh
                else:
                    stage[step + 1, block, rows, :] = fresh
            if comm and half == 2:
                @pl.when(not_last)
                def _():
                    border_copy().start()
            elif comm and step + 1 < STEPS:
                start_shift(step + 1, half)

        if comm:
            for kind in (0, 1, 2 + early):
                wait_latents(step, kind)
        def first(half, pair, rows):
            for row in rows:
                first_row(row, half, pair, x1, w1, act)

        def shape(half, pair, j):
            transform(half, pair, j, act, ust)

        window_columns(early, now, x1)
        low = 2 * early
        units = [(early, 0), (early, 1), (late, 0), (late, 1)]
        if step == 1:
            units = [units[0], units[2], units[1], units[3]]
        fresh_rows = (0, 1) if early else (4, 5)
        rows_of = [fresh_rows if half == late else (low, low + 2, low + 1, low + 3) for half, _ in units]
        windowed = [early]
        first(early, 0, rows_of[0])
        shape(early, 0, 0)
        for u, (half, pair) in enumerate(units):
            for j in range(4):
                if j in (1, 2) and u < 3:
                    if units[u + 1][0] not in windowed:
                        if comm:
                            if far_tile:
                                far_sends()
                            wait_latents(step, 2 + late)
                        window_columns(late, now, x1)
                        windowed.append(late)
                    rows = rows_of[u + 1]
                    first(*units[u + 1], rows[: len(rows) // 2] if j == 1 else rows[len(rows) // 2 :])
                product(half, pair, j, wt, ust, products)
                if j < 3:
                    shape(half, pair, j + 1)
                elif u < 3:
                    shape(*units[u + 1], 0)
                if j == 0 and u:
                    second_rows(*units[u - 1], products, held)
                if j == 1 and u:
                    term_rows(*units[u - 1], pst, held, sums)
                    if units[u - 1][1] == 0:
                        send_terms(units[u - 1][0])
                if u == 3 and j == 3:
                    finish(early)
        second_rows(*units[3], products, held)
        term_rows(*units[3], pst, held, sums)
        finish(late)

        if far_tile:
            if True:
                pltpu.make_async_copy(zeros, far, far_recv_sem).wait()
                window_columns(0, now, x1, far)
                first(0, 0, (0, 2, 1, 3))
                shape(0, 0, 0)
                for pair in range(2):
                    for j in range(4):
                        if pair == 0 and j in (1, 2):
                            first(0, 1, (0, 2) if j == 1 else (1, 3))
                        product(0, pair, j, wt, ust, products)
                        if j < 3:
                            shape(0, pair, j + 1)
                        elif pair == 0:
                            shape(0, 1, 0)
                        if pair and j == 0:
                            second_rows(0, 0, products, held, 2)
                        if pair and j == 1:
                            term_rows(2, 0, pst, held, sums)
                            send_terms(2)
                second_rows(0, 1, products, held, 2)
                term_rows(2, 1, pst, held, sums)
                finish(2)

    if comm:
        @pl.when(edge)
        def _():
            run(0, 1, True)

        @pl.when(jnp.logical_not(edge))
        def _():
            run(0, 0, False)
    else:
        run(0, 0, False)
    run(1, 1, False)

    for frame in range(4):
        for channel in range(4):
            out[frame, channel] = stage[STEPS, block_of(frame), pl.ds(channel, 4, stride=4), :].astype(BF16)

    if comm:
        for ok, copy in far_copies():
            @pl.when(ok)
            def _(copy=copy):
                copy.wait_send()

        @pl.when(redo)
        def _():
            for copy in term_copies(0, 2):
                copy.wait_send()

            @pl.when(not_last)
            def _():
                border_copy().wait_send()

        for step in range(STEPS):
            for half in range(2):
                for copy in term_copies(step, half):
                    copy.wait_send()

                @pl.when(not_last)
                def _(step=step, half=half):
                    main_copy(step, half).wait_send()

                    @pl.when(neighbour(half, step))
                    def _():
                        halo_copy(step, half).wait_send()

                @pl.when(first_level & neighbour(half))
                def _(step=step, half=half):
                    noise_copy(step, half).wait_send()


def call(levels, tiles, comm, *args):
    hbm = pl.BlockSpec(memory_space=pltpu.HBM)
    smem = pl.BlockSpec(memory_space=pltpu.SMEM)
    scratch = [
        pltpu.VMEM((4, 4, 4, COLS), BF16),
        pltpu.VMEM((2, 4, 4, 4, COLS), BF16),
        pltpu.VMEM((9, 4, CH), BF16),
        pltpu.VMEM((9, CH, CH), BF16),
        pltpu.VMEM((3, CH, CH), BF16),
        pltpu.VMEM((4, CH), BF16),
        pltpu.VMEM((4, CH, 3 * CH), BF16),
        pltpu.VMEM((COLS, 384), F32),
        pltpu.VMEM((6 * CH, COLS), BF16),
        pltpu.VMEM((16, CH), F32),
        pltpu.VMEM((2, 32, 704), F32),
        pltpu.VMEM((STEPS, 4, 32, COLS), F32),
        pltpu.VMEM((STEPS + 1, 4, 16, COLS), F32),
        pltpu.VMEM((STEPS, 4, 16, COLS), F32),
        pltpu.VMEM((4, 8, COLS), F32),
        pltpu.VMEM((2, 96, 512), BF16),
        pltpu.VMEM((2, 6, CH, 256), BF16),
        pltpu.VMEM((2, 2, 4, 3 * CH, 256), BF16),
        pltpu.VMEM((2, 2, 4, CH, 256), F32),
        pltpu.VMEM((3, 2, 2, 704, 256), BF16),
        pltpu.VMEM((3, 2, 3, 8, 256), F32),
        pltpu.VMEM((STEPS, 3, 8, COLS), F32),
        pltpu.VMEM((STEPS, 3, 8, COLS), F32),
        pltpu.VMEM((STEPS, 3, 8, COLS), F32),
        pltpu.VMEM((STEPS, 3, 8, COLS), F32),
        pltpu.SemaphoreType.DMA((6,)),
        pltpu.SemaphoreType.DMA((STEPS, 6)),
        pltpu.SemaphoreType.DMA((STEPS, 4)),
        pltpu.SemaphoreType.DMA((STEPS, 3, 2)),
        pltpu.SemaphoreType.DMA((STEPS, 3, 2)),
        pltpu.SemaphoreType.REGULAR,
        pltpu.VMEM((4, 8, COLS), F32),
        pltpu.VMEM((4, 8, COLS), F32),
        pltpu.SemaphoreType.DMA((3,)),
        pltpu.SemaphoreType.DMA,
    ]
    return pl.pallas_call(
        functools.partial(kernel, levels, tiles, comm),
        out_shape=jax.ShapeDtypeStruct((4, 4, 4, COLS), BF16),
        in_specs=[hbm] * 6 + [smem] * 2,
        out_specs=pl.BlockSpec(memory_space=pltpu.VMEM),
        scratch_shapes=scratch,
        compiler_params=pltpu.CompilerParams(
            vmem_limit_bytes=62 << 20,
            **(dict(collective_id=0, has_side_effects=True) if comm else {}),
        ),
        name="queue_steps",
    )(*args)


def per_device(levels, tiles, queue_init, noise_frames, conv_first, conv_second, time_weight, out_proj, keep_coef, noise_coef):
    out = call(
        levels, tiles, True, queue_init[0], noise_frames, jnp.transpose(conv_first, (0, 1, 3, 2)).reshape(9, 4, CH), conv_second.reshape(9, CH, CH),
        time_weight, out_proj, keep_coef, noise_coef,
    )
    return out[None]


def solution(mesh):
    return jax.shard_map(
        functools.partial(per_device, mesh.shape["level"], mesh.shape["tile"]),
        mesh=mesh,
        in_specs=(
            P("level", None, None, "tile", None),
            P(None, None, None, "tile", None),
            P(),
            P(),
            P(),
            P(),
            P(),
            P(),
        ),
        out_specs=P("level", None, None, "tile", None),
        check_vma=False,
    )
```

```python
import functools

import jax
import jax.numpy as jnp
from jax import lax
from jax.experimental import pallas as pl
from jax.experimental.pallas import tpu as pltpu
from jax.sharding import PartitionSpec as P

STEPS = 2
CH = 320
COLS = 128
ORDER = (0, 3, 1, 2)
F32 = jnp.float32
BF16 = jnp.bfloat16
MESH = pl.DeviceIdType.MESH


def block_of(frame):
    return ORDER.index(frame)


def shifted_cols(value, amount):
    lane = lax.broadcasted_iota(jnp.int32, value.shape, 1)
    rolled = pltpu.roll(value, amount % COLS, 1)
    edge = 0 if amount == 1 else COLS - 1
    return jnp.where(lane == edge, jnp.zeros_like(rolled), rolled)


def spread(source, index, target):
    for frame in range(4):
        for channel in range(4):
            piece = source[index + (frame, channel)].astype(F32)
            target[block_of(frame), pl.ds(channel, 4, stride=4), :] = piece


def prepare_first(cf, w1t, w1, top_mask, bottom_mask):
    w1t[...] = jnp.zeros_like(w1t)
    for row_tap in range(3):
        for col_tap in range(3):
            place = col_tap * 32 + row_tap * 4
            w1t[place : place + 4, 0:CH] = cf[row_tap * 3 + col_tap].astype(F32) * 0.5
    base = jnp.transpose(w1t[...])[0:CH]
    for row in range(6):
        value = pltpu.roll(base, 4 * row, 1) if row else base
        if row == 0:
            value = value * top_mask
        if row == 5:
            value = value * bottom_mask
        w1[row * CH : (row + 1) * CH, :] = value.astype(BF16)


def prepare_second(cs, wt):
    for col_tap in range(3):
        lanes = slice(col_tap * CH, (col_tap + 1) * CH)
        g0, g1, g2 = (cs[a * 3 + col_tap].astype(F32) for a in range(3))
        outer = 0.25 * (g0 + g2)
        wt[0, :, lanes] = (0.5 * g0).astype(BF16)
        wt[1, :, lanes] = (outer + 0.25 * g1).astype(BF16)
        wt[2, :, lanes] = (outer - 0.25 * g1).astype(BF16)
        wt[3, :, lanes] = (0.5 * g2).astype(BF16)


def prepare_projection(op, tw, p16, pst):
    p16[...] = jnp.zeros_like(p16)
    p16[0:4, :] = op[...].astype(F32)
    p16[12:16, :] = op[...].astype(F32)
    both = p16[...].astype(BF16)
    pst[...] = jnp.zeros_like(pst)
    through = [jnp.dot(both, tw[k], preferred_element_type=F32) for k in range(3)]
    for odd in range(2):
        rows = slice(odd * 8, odd * 8 + 8)
        pst[odd, 0:8, 0:CH] = p16[rows, :] * 2.0
        for place, k in enumerate((1, 0, 2)):
            pst[odd, place * 8 : place * 8 + 8, 384 : 384 + CH] = through[k][rows]


def window_columns(half, q, x1, far=None):
    for block in range(4):
        lanes = slice(block * COLS, (block + 1) * COLS)
        if far is not None:
            value = jnp.concatenate([far[block], q[block, 0:16, :], jnp.zeros((8, COLS), F32)], axis=0)
        elif half == 0:
            value = jnp.concatenate([q[block, 0:24, :], jnp.zeros((8, COLS), F32)], axis=0)
        else:
            value = jnp.concatenate([jnp.zeros((8, COLS), F32), q[block, 8:32, :]], axis=0)
        x1[half, 0:32, lanes] = shifted_cols(value, 1).astype(BF16)
        x1[half, 32:64, lanes] = value.astype(BF16)
        x1[half, 64:96, lanes] = shifted_cols(value, -1).astype(BF16)


def first_row(row, half, pair, x1, w1, act):
    part = jnp.dot(
        w1[row * CH : (row + 1) * CH, 0:96], x1[half, :, pair * 256 : pair * 256 + 256], preferred_element_type=F32
    )
    act[pair, row] = (part + part * jnp.tanh(part)).astype(BF16)


def transform(half, pair, j, act, ust):
    left, right = ((0, 2), (1, 2), (2, 1), (1, 3))[j]
    for block in range(2):
        lanes = slice(block * COLS, (block + 1) * COLS)
        one = act[pair, 2 * half + left, :, lanes]
        two = act[pair, 2 * half + right, :, lanes]
        piece = one + two if j == 1 else one - two
        ust[half, pair, j, 0:CH, lanes] = shifted_cols(piece, 1)
        ust[half, pair, j, CH : 2 * CH, lanes] = piece
        ust[half, pair, j, 2 * CH : 3 * CH, lanes] = shifted_cols(piece, -1)


def product(half, pair, j, wt, ust, products):
    products[half, pair, j] = jnp.dot(wt[j], ust[half, pair, j], preferred_element_type=F32)


def second_rows(half, pair, products, held, slot=None):
    slot = half if slot is None else slot
    for odd in range(2):
        one, two = products[half, pair, 1], products[half, pair, 2]
        value = products[half, pair, 0] + one + two if odd == 0 else one - two - products[half, pair, 3]
        held[slot, pair, odd, 0:CH, :] = value.astype(BF16)
        held[slot, pair, odd, 384 : 384 + CH, :] = (value + value * jnp.tanh(value)).astype(BF16)


def term_rows(half, pair, pst, held, sums):
    terms = [
        jnp.dot(pst[odd].astype(BF16), held[half, pair, odd], preferred_element_type=F32) for odd in range(2)
    ]
    total = terms[0] + terms[1]
    for place in range(3):
        sums[half, pair, place] = total[place * 8 : place * 8 + 8]


def part_of(sums, half, place, frame):
    block = block_of(frame)
    return sums[half, block // 2, place, :, (block % 2) * COLS : (block % 2 + 1) * COLS]


def kernel(levels, tiles, comm, queue_hbm, noise_hbm, cf_hbm, cs_hbm, tw_hbm, op_hbm, keep, rate, out,
           qin, nin, cf, cs, tw, op, wt, w1t, w1, p16, pst, q, stage, noise, zeros, x1, act, ust, products, held, sums,
           lo_send, hi_send, lo_recv, hi_recv, load_sem, send_sem, recv_sem, term_send_sem, term_recv_sem,
           far_ready, far, border, far_send_sem, far_recv_sem):
    if comm:
        g, t = lax.axis_index("level"), lax.axis_index("tile")
    else:
        g, t = jnp.int32(0), jnp.int32(1)
    has_up, has_down = t > 0, t < tiles - 1
    first_level, not_last = g == 0, g < levels - 1
    period = max(tiles // 4, 1)
    edge = has_up & (lax.rem(t, period) == 0)
    next_edge = has_down & (lax.rem(t + 1, period) == 0)
    redo, next_redo = edge, next_edge

    loads = [
        pltpu.make_async_copy(source, target, load_sem.at[i])
        for i, (source, target) in enumerate(
            [(queue_hbm, qin), (noise_hbm, nin), (cf_hbm, cf), (op_hbm, op), (tw_hbm, tw), (cs_hbm, cs)]
        )
    ]
    for load in loads:
        load.start()

    if comm:
        barrier = pltpu.get_barrier_semaphore()
        count = jnp.int32(0)
        for dg in (-1, 0, 1):
            for dt in (-1, 0, 1):
                if dg == 0 and dt == 0:
                    continue
                ok = (t + dt >= 0) & (t + dt < tiles)
                if dg == 0:
                    ok = ok & first_level

                @pl.when(ok & jnp.logical_not(next_edge) if dt == 1 else ok)
                def _(dg=dg, dt=dt):
                    pl.semaphore_signal(
                        barrier, inc=1, device_id=(lax.rem(g + dg + levels, levels), t + dt), device_id_type=MESH
                    )

                counted = ok & jnp.logical_not(edge) if dt == -1 else ok
                count = count + counted.astype(jnp.int32)

    loads[0].wait()
    spread(qin, (), stage.at[0])
    zeros[...] = jnp.zeros_like(zeros)

    def place(step, kind):
        start = (8, 16, 0, 24)[kind]
        return q.at[step, :, start : start + 8, :]

    def remote(source, step, kind, level, tile, send):
        return pltpu.make_async_remote_copy(
            src_ref=source, dst_ref=place(step, kind), send_sem=send_sem.at[step, send],
            recv_sem=recv_sem.at[step, kind], device_id=(level, tile), device_id_type=MESH,
        )

    def main_copy(step, half):
        return remote(stage.at[step, :, 8 * half : 8 * half + 8, :], step, half, g + 1, t, half)

    def halo_copy(step, half):
        source = stage.at[step, :, 8 * half : 8 * half + 8, :]
        return remote(source, step, 3 - half, g + 1, t + (1 if half else -1), 2 + half)

    def noise_copy(step, half):
        source = noise.at[step, :, 8 * half : 8 * half + 8, :]
        return remote(source, step, 3 - half, g, t + (1 if half else -1), 4 + half)

    def local_copy(source, step, kind):
        return pltpu.make_async_copy(source, place(step, kind), recv_sem.at[step, kind])

    def term_copies(step, half):
        return [
            pltpu.make_async_remote_copy(
                src_ref=source.at[step, half], dst_ref=target.at[step, half], send_sem=term_send_sem.at[step, half, i],
                recv_sem=term_recv_sem.at[step, half, i], device_id=(lax.rem(g + dg, levels), t), device_id_type=MESH,
            )
            for i, (source, target, dg) in enumerate([(lo_send, hi_recv, levels - 1), (hi_send, lo_recv, 1)])
        ]

    def neighbour(half, step=0):
        if half and step:
            return has_down & jnp.logical_not(next_redo)
        return has_down if half else has_up

    def far_copy(source, level, send):
        return pltpu.make_async_remote_copy(
            src_ref=source, dst_ref=far, send_sem=far_send_sem.at[send], recv_sem=far_recv_sem,
            device_id=(level, t + 1), device_id_type=MESH,
        )

    def far_copies():
        return [
            (next_redo & not_last, far_copy(stage.at[0, :, 0:8, :], g + 1, 0)),
            (next_redo & first_level, far_copy(noise.at[0, :, 0:8, :], 0 * g, 1)),
        ]

    def border_copy():
        return pltpu.make_async_remote_copy(
            src_ref=border, dst_ref=place(1, 2), send_sem=far_send_sem.at[2], recv_sem=recv_sem.at[1, 2],
            device_id=(g + 1, t), device_id_type=MESH,
        )

    def start_shift(step, half):
        @pl.when(not_last)
        def _():
            main_copy(step, half).start()

            @pl.when(neighbour(half) & jnp.logical_not(edge) if step == 0 and half == 0 else neighbour(half, step))
            def _():
                halo_copy(step, half).start()

    def far_sends():
        pl.semaphore_wait(far_ready, 2 + first_level.astype(jnp.int32))

        @pl.when(not_last)
        def _():
            halo_copy(0, 0).start()

        @pl.when(first_level)
        def _():
            for step in range(STEPS):
                noise_copy(step, 0).start()

    def wait_latents(step, kind):
        local_copy(zeros, step, kind).wait()

    if comm:
        pl.semaphore_wait(barrier, count)
        for dg in (-1, 0, 1):
            @pl.when(next_edge & first_level if dg == 0 else next_edge)
            def _(dg=dg):
                pl.semaphore_signal(
                    far_ready, inc=1, device_id=(lax.rem(g + dg + levels, levels), t + 1), device_id_type=MESH
                )

        for half in (1, 0):
            start_shift(0, half)
        loads[1].wait()

        @pl.when(first_level)
        def _():
            for step in range(STEPS):
                spread(nin, (step,), noise.at[step])
                for half in range(2):
                    local_copy(noise.at[step, :, 8 * half : 8 * half + 8, :], step, half).start()

        for half in range(2):
            @pl.when(jnp.logical_not(neighbour(half)))
            def _(half=half):
                for step in range(STEPS):
                    local_copy(zeros, step, 2 + half).start()

        for half in (1, 0):
            @pl.when(first_level & neighbour(half) & (jnp.logical_not(edge) if half == 0 else has_down))
            def _(half=half):
                for step in range(STEPS):
                    noise_copy(step, half).start()

        for ok, copy in far_copies():
            @pl.when(ok)
            def _(copy=copy):
                copy.start()

    if not comm:
        loads[1].wait()
    for half in range(3):
        for pair in range(2):
            for odd in range(2):
                held[half, pair, odd, CH:384, :] = jnp.zeros((64, 256), BF16)
    loads[2].wait()
    prepare_first(cf, w1t, w1, has_up.astype(F32), has_down.astype(F32))
    loads[3].wait()
    loads[4].wait()
    loads[5].wait()
    prepare_second(cs, wt)

    lo_mask, hi_mask = (g > 0).astype(F32), not_last.astype(F32)
    def run(step, early, far_tile):
        now = q.at[step]
        late = 1 - early

        def send_terms(half):
            lo_send[step, half] = part_of(sums, half, 2, 0)
            hi_send[step, half] = part_of(sums, half, 1, 3)
            if comm:
                for copy in term_copies(step, half):
                    copy.start()

        def finish(half):
            if comm:
                for copy in term_copies(step, half):
                    copy.wait_recv()
            rows = slice(8 * half, 8 * half + 8)
            for frame in range(4):
                block = block_of(frame)
                before = lo_recv[step, half] * lo_mask if frame == 0 else part_of(sums, half, 1, frame - 1)
                after = hi_recv[step, half] * hi_mask if frame == 3 else part_of(sums, half, 2, frame + 1)
                projected = part_of(sums, half, 0, frame) + before + after
                latent = now[block, 0:8, :] if half == 2 else now[block, 8 + 8 * half : 16 + 8 * half, :]
                fresh = keep[step, g, frame] * latent - rate[step, g, frame] * projected
                fresh = fresh.astype(BF16).astype(F32)
                if half == 2:
                    border[block] = fresh
                else:
                    stage[step + 1, block, rows, :] = fresh
            if comm and half == 2:
                @pl.when(not_last)
                def _():
                    border_copy().start()
            elif comm and step + 1 < STEPS:
                start_shift(step + 1, half)

        if comm:
            for kind in (0, 1, 2 + early):
                wait_latents(step, kind)
        def first(half, pair, rows):
            for row in rows:
                first_row(row, half, pair, x1, w1, act)

        def shape(half, pair, j):
            transform(half, pair, j, act, ust)

        window_columns(early, now, x1)
        low = 2 * early
        units = [(early, 0), (early, 1), (late, 0), (late, 1)]
        if step == 1:
            units = [units[0], units[2], units[1], units[3]]
        fresh_rows = (0, 1) if early else (4, 5)
        rows_of = [fresh_rows if half == late else (low, low + 2, low + 1, low + 3) for half, _ in units]
        windowed = [early]
        first(early, 0, rows_of[0])
        shape(early, 0, 0)
        for u, (half, pair) in enumerate(units):
            for j in range(4):
                if j in (1, 2) and u < 3:
                    if units[u + 1][0] not in windowed:
                        if comm:
                            if far_tile:
                                far_sends()
                            wait_latents(step, 2 + late)
                        window_columns(late, now, x1)
                        windowed.append(late)
                    rows = rows_of[u + 1]
                    first(*units[u + 1], rows[: len(rows) // 2] if j == 1 else rows[len(rows) // 2 :])
                product(half, pair, j, wt, ust, products)
                if j < 3:
                    shape(half, pair, j + 1)
                elif u < 3:
                    shape(*units[u + 1], 0)
                if step == 0 and u == 0 and j == 3:
                    prepare_projection(op, tw, p16, pst)
                if j == 0 and u:
                    second_rows(*units[u - 1], products, held)
                if j == 1 and u:
                    term_rows(*units[u - 1], pst, held, sums)
                    if units[u - 1][1] == 0:
                        send_terms(units[u - 1][0])
                if u == 3 and j == 2:
                    finish(early)
        second_rows(*units[3], products, held)
        term_rows(*units[3], pst, held, sums)
        finish(late)

        if far_tile:
            if True:
                pltpu.make_async_copy(zeros, far, far_recv_sem).wait()
                window_columns(0, now, x1, far)
                first(0, 0, (0, 2, 1, 3))
                shape(0, 0, 0)
                for pair in range(2):
                    for j in range(4):
                        if pair == 0 and j in (1, 2):
                            first(0, 1, (0, 2) if j == 1 else (1, 3))
                        product(0, pair, j, wt, ust, products)
                        if j < 3:
                            shape(0, pair, j + 1)
                        elif pair == 0:
                            shape(0, 1, 0)
                        if pair and j == 0:
                            second_rows(0, 0, products, held, 2)
                        if pair and j == 1:
                            term_rows(2, 0, pst, held, sums)
                            send_terms(2)
                second_rows(0, 1, products, held, 2)
                term_rows(2, 1, pst, held, sums)
                finish(2)

    if comm:
        @pl.when(edge)
        def _():
            run(0, 1, True)

        @pl.when(jnp.logical_not(edge))
        def _():
            run(0, 0, False)
    else:
        run(0, 0, False)
    run(1, 1, False)

    for frame in range(4):
        for channel in range(4):
            out[frame, channel] = stage[STEPS, block_of(frame), pl.ds(channel, 4, stride=4), :].astype(BF16)

    if comm:
        for ok, copy in far_copies():
            @pl.when(ok)
            def _(copy=copy):
                copy.wait_send()

        @pl.when(redo)
        def _():
            for copy in term_copies(0, 2):
                copy.wait_send()

            @pl.when(not_last)
            def _():
                border_copy().wait_send()

        for step in range(STEPS):
            for half in range(2):
                for copy in term_copies(step, half):
                    copy.wait_send()

                @pl.when(not_last)
                def _(step=step, half=half):
                    main_copy(step, half).wait_send()

                    @pl.when(neighbour(half, step))
                    def _():
                        halo_copy(step, half).wait_send()

                @pl.when(first_level & neighbour(half))
                def _(step=step, half=half):
                    noise_copy(step, half).wait_send()


def call(levels, tiles, comm, *args):
    hbm = pl.BlockSpec(memory_space=pltpu.HBM)
    smem = pl.BlockSpec(memory_space=pltpu.SMEM)
    scratch = [
        pltpu.VMEM((4, 4, 4, COLS), BF16),
        pltpu.VMEM((2, 4, 4, 4, COLS), BF16),
        pltpu.VMEM((9, 4, CH), BF16),
        pltpu.VMEM((9, CH, CH), BF16),
        pltpu.VMEM((3, CH, CH), BF16),
        pltpu.VMEM((4, CH), BF16),
        pltpu.VMEM((4, CH, 3 * CH), BF16),
        pltpu.VMEM((COLS, 384), F32),
        pltpu.VMEM((6 * CH, COLS), BF16),
        pltpu.VMEM((16, CH), F32),
        pltpu.VMEM((2, 32, 704), F32),
        pltpu.VMEM((STEPS, 4, 32, COLS), F32),
        pltpu.VMEM((STEPS + 1, 4, 16, COLS), F32),
        pltpu.VMEM((STEPS, 4, 16, COLS), F32),
        pltpu.VMEM((4, 8, COLS), F32),
        pltpu.VMEM((2, 96, 512), BF16),
        pltpu.VMEM((2, 6, CH, 256), BF16),
        pltpu.VMEM((2, 2, 4, 3 * CH, 256), BF16),
        pltpu.VMEM((2, 2, 4, CH, 256), F32),
        pltpu.VMEM((3, 2, 2, 704, 256), BF16),
        pltpu.VMEM((3, 2, 3, 8, 256), F32),
        pltpu.VMEM((STEPS, 3, 8, COLS), F32),
        pltpu.VMEM((STEPS, 3, 8, COLS), F32),
        pltpu.VMEM((STEPS, 3, 8, COLS), F32),
        pltpu.VMEM((STEPS, 3, 8, COLS), F32),
        pltpu.SemaphoreType.DMA((6,)),
        pltpu.SemaphoreType.DMA((STEPS, 6)),
        pltpu.SemaphoreType.DMA((STEPS, 4)),
        pltpu.SemaphoreType.DMA((STEPS, 3, 2)),
        pltpu.SemaphoreType.DMA((STEPS, 3, 2)),
        pltpu.SemaphoreType.REGULAR,
        pltpu.VMEM((4, 8, COLS), F32),
        pltpu.VMEM((4, 8, COLS), F32),
        pltpu.SemaphoreType.DMA((3,)),
        pltpu.SemaphoreType.DMA,
    ]
    return pl.pallas_call(
        functools.partial(kernel, levels, tiles, comm),
        out_shape=jax.ShapeDtypeStruct((4, 4, 4, COLS), BF16),
        in_specs=[hbm] * 6 + [smem] * 2,
        out_specs=pl.BlockSpec(memory_space=pltpu.VMEM),
        scratch_shapes=scratch,
        compiler_params=pltpu.CompilerParams(
            vmem_limit_bytes=62 << 20,
            **(dict(collective_id=0, has_side_effects=True) if comm else {}),
        ),
        name="queue_steps",
    )(*args)


def per_device(levels, tiles, queue_init, noise_frames, conv_first, conv_second, time_weight, out_proj, keep_coef, noise_coef):
    out = call(
        levels, tiles, True, queue_init[0], noise_frames, jnp.transpose(conv_first, (0, 1, 3, 2)).reshape(9, 4, CH), conv_second.reshape(9, CH, CH),
        time_weight, out_proj, keep_coef, noise_coef,
    )
    return out[None]


def solution(mesh):
    return jax.shard_map(
        functools.partial(per_device, mesh.shape["level"], mesh.shape["tile"]),
        mesh=mesh,
        in_specs=(
            P("level", None, None, "tile", None),
            P(None, None, None, "tile", None),
            P(),
            P(),
            P(),
            P(),
            P(),
            P(),
        ),
        out_specs=P("level", None, None, "tile", None),
        check_vma=False,
    )
```
